512 devices in a mesh: gx: 16 (over z_lo, core), gy: 32 (over z_hi, y, x).
Axes of the slice: x: 4, y: 4, z: 16 (z_hi: 2, z_lo: 8; z = z_hi * 8 + z_lo), core: 2. Of those that a mesh axis runs over, the one named last changes fastest.
Arguments:
- leaf_raw: float32 [16, 32, 768, 768], P('gx', 'gy'), may hold values from -32 to 80, as said below
- medium_class: int32 [16, 32, 12], P('gx', 'gy'), may hold values from 0 to 7
- wave_table: float32 [8], replicated, may hold values from 1 to 4
- boundary_data: float32 [16, 32, 384, 128], P('gx', 'gy'), may hold values from -6 to 6
Outputs:
- parent_rows: float32 [16, 32, 384, 1536], P('gx', 'gy')
- interface_values: float32 [16, 32, 384, 128], P('gx', 'gy')
The draws below stay inside these ranges and needn't reach their ends.
Inputs may be any that keep to these rules, and one draw needn't show every extreme that they name: Each tile's block leaf_raw[p, q] is symmetric positive semidefinite.
All inputs are finite; a program needn't handle non-finite values.
Results may differ from the reference program's by a relative error of at most 0.0001.
Values sent between devices are 32-bit elements; how exact they have to be, the bound alone decides.
A program may use at most 64 MiB of HBM per device.

```python
import math
import jax
import jax.numpy as jnp
from jax import lax

SIDE = 192
BOUND = 768
NCOL = 128
BLK = 64
NBLK = 12
NCLS = 8
N_GX = 16
N_GY = 32


def side_kernel():
    amplitude = 24.0
    kernel_width = 8.0
    points = jnp.arange(BOUND, dtype=jnp.int32)
    side_index = points // SIDE
    along = (points % SIDE).astype(jnp.float32)
    distance = (along[:, None] - along[None, :]) / kernel_width
    same_side = (side_index[:, None] == side_index[None, :]).astype(jnp.float32)
    return amplitude * jnp.exp(-distance * distance) * same_side


def draw_leaf_raw(key, part):
    tile_count = N_GX * N_GY
    coupling = 16.0
    smooth_part = side_kernel()

    def one_tile(tile_index):
        tile_key = jax.random.fold_in(key, tile_index)
        factor_draw = jax.random.normal(tile_key, (BOUND, BOUND), jnp.float32)
        wishart = jnp.dot(factor_draw, factor_draw.T, precision=lax.Precision.HIGHEST, preferred_element_type=jnp.float32) * (coupling / BOUND)
        return wishart + smooth_part
    tile_maps = lax.map(one_tile, jnp.arange(tile_count, dtype=jnp.int32))
    return tile_maps.reshape(N_GX, N_GY, BOUND, BOUND)


def touch_ends(drawn, key, low, largest):
    extent = drawn.shape
    spot = [jax.random.randint(jax.random.fold_in(key, axis), (), 0, extent[axis]) for axis in range(len(extent))]
    drawn = drawn.at[tuple(spot)].set(low)
    longest = extent.index(max(extent))
    spot[longest] = (spot[longest] + 1) % extent[longest]
    return drawn.at[tuple(spot)].set(largest)


def level_of(stream_key, dims, cuts, smallest, largest):
    loudness, own = 1.0, jax.random.fold_in(stream_key, 6)
    for position, blocks in cuts:
        steps = jnp.exp(jax.random.uniform(jax.random.fold_in(own, position), (blocks,), jnp.float32, smallest / len(cuts), largest / len(cuts)))
        loudness = loudness * jnp.repeat(steps, dims[position] // blocks).reshape([-1 if axis == position else 1 for axis in range(len(dims))])
    return loudness


def noise(key, dims, spread, limit, shards=(), held_as=jnp.bfloat16):
    loudness = level_of(key, dims, shards, -0.22, 0.18) if shards else 1.0
    result = jax.random.normal(key, dims, jnp.float32) * spread * loudness
    return jnp.minimum(jnp.maximum(result, -limit), limit).astype(held_as)


def setup_inputs(seed: int = 0) -> dict:
    streams_of = jax.random.split(jax.random.key(seed), 5)
    leaf_raw = draw_leaf_raw(jax.random.fold_in(streams_of[4], 71), 0)
    medium_class = touch_ends(jax.random.randint(streams_of[1], (N_GX, N_GY, NBLK), 0, NCLS), jax.random.fold_in(streams_of[1], 1), 0, NCLS - 1).astype(jnp.int32)
    wave_table = jnp.clip(jnp.exp(jax.random.uniform(streams_of[2], (NCLS,), jnp.float32, math.log(1.0), math.log(4.0))), 1.0, 4.0)
    boundary_data = noise(streams_of[3], (N_GX, N_GY, 2 * SIDE, NCOL), 1.0, 6.0, ((0, 16), (1, 32)), jnp.float32)
    return {"leaf_raw": leaf_raw, "medium_class": medium_class, "wave_table": wave_table, "boundary_data": boundary_data}


highest = lax.Precision.HIGHEST

def product(left_mat, right_mat):
    return jnp.dot(left_mat.astype(jnp.float32), right_mat.astype(jnp.float32), precision=highest, preferred_element_type=jnp.float32)

def inner_product(left_mat, right_mat):
    return lax.dot_general(left_mat.astype(jnp.float32), right_mat.astype(jnp.float32), (((0,), (0,)), ((), ())), precision=highest, preferred_element_type=jnp.float32)

def lower_solve(factor, right_side):
    return lax.linalg.triangular_solve(factor, right_side, left_side=True, lower=True)

def upper_solve(factor, right_side):
    return lax.linalg.triangular_solve(factor, right_side, left_side=True, lower=True, transpose_a=True)

def level_outer(matrix, side_len):
    return jnp.concatenate([matrix[:, :2 * side_len], matrix[:, 3 * side_len:5 * side_len]], axis=1)

def level_inner(matrix, side_len):
    return jnp.concatenate([matrix[:, 2 * side_len:3 * side_len], matrix[:, 5 * side_len:]], axis=1)

def build_leaf(raw_block, classes, wave_table):
    diagonal = 4.0 + jnp.repeat(wave_table[classes], BLK)
    return 0.5 * (raw_block + raw_block.T) + jnp.diag(diagonal)

def merge_one(lower_leaf, upper_leaf):
    exterior = 3 * SIDE
    factor = jnp.linalg.cholesky(lower_leaf[exterior:, exterior:] + upper_leaf[exterior:, exterior:])
    solved = lower_solve(factor, jnp.concatenate([lower_leaf[exterior:, :exterior], upper_leaf[exterior:, :exterior]], axis=1))
    zero_block = jnp.zeros((exterior, exterior), jnp.float32)
    blocks = jnp.concatenate([jnp.concatenate([lower_leaf[:exterior, :exterior], zero_block], axis=1), jnp.concatenate([zero_block, upper_leaf[:exterior, :exterior]], axis=1)], axis=0)
    return (blocks - inner_product(solved, solved), factor, solved)

def rows_inner(matrix):
    return jnp.concatenate([matrix[2 * SIDE:3 * SIDE], matrix[5 * SIDE:]], axis=0)

def rows_outer(matrix):
    return jnp.concatenate([matrix[:2 * SIDE], matrix[3 * SIDE:5 * SIDE]], axis=0)

def merge_two(lower_parent, upper_parent):
    face_lower = rows_inner(lower_parent)
    face_upper = rows_inner(upper_parent)
    factor = jnp.linalg.cholesky(level_inner(face_lower, SIDE) + level_inner(face_upper, SIDE))
    solved = lower_solve(factor, jnp.concatenate([level_outer(face_lower, SIDE), level_outer(face_upper, SIDE)], axis=1))
    zero_block = jnp.zeros((4 * SIDE, 4 * SIDE), jnp.float32)
    blocks = jnp.concatenate([jnp.concatenate([level_outer(rows_outer(lower_parent), SIDE), zero_block], axis=1), jnp.concatenate([zero_block, level_outer(rows_outer(upper_parent), SIDE)], axis=1)], axis=0)
    return (blocks - inner_product(solved, solved), factor, solved)

def group_work(tiles_raw, tiles_class, wave_table, tiles_data):
    parents = []
    factors = []
    solveds = []
    for row_half in range(2):
        lower_leaf = build_leaf(tiles_raw[0, row_half], tiles_class[0, row_half], wave_table)
        upper_leaf = build_leaf(tiles_raw[1, row_half], tiles_class[1, row_half], wave_table)
        parent, factor, solved = merge_one(lower_leaf, upper_leaf)
        parents.append(parent)
        factors.append(factor)
        solveds.append(solved)
    top_map, factor_two, solved_two = merge_two(parents[0], parents[1])
    rows_four = jnp.swapaxes(top_map.reshape(2, 2, 2 * SIDE, 8 * SIDE), 0, 1)
    stacked = jnp.concatenate([tiles_data[0, 0], tiles_data[1, 0], tiles_data[0, 1], tiles_data[1, 1]], axis=0)
    gy_values = -upper_solve(factor_two, product(solved_two, stacked))
    columns = []
    for row_half in range(2):
        first_part = jnp.concatenate([tiles_data[0, row_half], gy_values[:SIDE]], axis=0)
        second_part = jnp.concatenate([tiles_data[1, row_half], gy_values[SIDE:]], axis=0)
        gx_values = -upper_solve(factors[row_half], product(solveds[row_half], jnp.concatenate([first_part, second_part], axis=0)))
        columns.append(jnp.stack([jnp.concatenate([gy_values[:SIDE], gx_values], axis=0), jnp.concatenate([gy_values[SIDE:], gx_values], axis=0)], axis=0))
    values_four = jnp.stack(columns, axis=1)
    return (rows_four, values_four)

def take_group(array, first_row, second_row):
    half_x = N_GX // 2
    half_y = N_GY // 2
    rest = array.shape[2:]
    anchor = tuple((jnp.int32(0) for _ in rest))
    outer_list = []
    for kx in range(2):
        inner_list = []
        for ky in range(2):
            start = (jnp.int32(first_row + kx * half_x), jnp.int32(second_row + ky * half_y)) + anchor
            inner_list.append(lax.dynamic_slice(array, start, (1, 1) + rest)[0, 0])
        outer_list.append(jnp.stack(inner_list, axis=0))
    return jnp.stack(outer_list, axis=0)

def put_group(array, group_vals, first_row, second_row):
    half_x = N_GX // 2
    half_y = N_GY // 2
    anchor = tuple((jnp.int32(0) for _ in array.shape[2:]))
    for kx in range(2):
        for ky in range(2):
            start = (jnp.int32(first_row + kx * half_x), jnp.int32(second_row + ky * half_y)) + anchor
            array = lax.dynamic_update_slice(array, group_vals[kx, ky][None, None], start)
    return array

def reference(leaf_raw, medium_class, wave_table, boundary_data):
    half_x = N_GX // 2
    half_y = N_GY // 2
    groups = half_x * half_y

    def group_step(group_index, state_pair):
        rows_all, values_all = state_pair
        group_index = jnp.asarray(group_index).astype(jnp.int32)
        first_row = (group_index // half_y).astype(jnp.int32)
        second_row = (group_index % half_y).astype(jnp.int32)
        tiles_raw = take_group(leaf_raw, first_row, second_row)
        tiles_class = take_group(medium_class, first_row, second_row)
        tiles_data = take_group(boundary_data, first_row, second_row)
        rows_four, values_four = group_work(tiles_raw, tiles_class, wave_table, tiles_data)
        rows_all = put_group(rows_all, rows_four, first_row, second_row)
        values_all = put_group(values_all, values_four, first_row, second_row)
        return (rows_all, values_all)
    start_state = (jnp.zeros((N_GX, N_GY, 2 * SIDE, 8 * SIDE), jnp.float32), jnp.zeros((N_GX, N_GY, 2 * SIDE, NCOL), jnp.float32))
    parent_rows, interface_values = lax.fori_loop(0, groups, group_step, start_state)
    return (parent_rows, interface_values)
```

```python
import functools

import jax
import jax.numpy as jnp
from jax import lax
from jax.experimental import pallas as pl
from jax.experimental.pallas import tpu as pltpu
from jax.sharding import PartitionSpec as P

highest = lax.Precision.HIGHEST
MESH = pl.DeviceIdType.MESH
T = 128
f32 = jnp.float32


def product(left, right):
    return jnp.dot(left, right, precision=highest, preferred_element_type=f32)


def inner(left, right):
    return lax.dot_general(
        left, right, (((0,), (0,)), ((), ())), precision=highest, preferred_element_type=f32
    )


def invert_tile(ref):
    lane = lax.broadcasted_iota(jnp.int32, (8, T), 1)
    sub = lax.broadcasted_iota(jnp.int32, (8, T), 0)
    wide_lane = lax.broadcasted_iota(jnp.int32, (T, T), 1)

    def step(k, carry):
        start = pl.multiple_of(k * 8, 8)
        panel = ref[pl.ds(start, 8), :]
        for j in range(8):
            column = jnp.broadcast_to(panel[:, j : j + 1], (8, T))
            row = jnp.broadcast_to(panel[j : j + 1, :], (8, T))
            pivot = jnp.broadcast_to(panel[j : j + 1, j : j + 1], (8, T))
            scaled = jnp.where(lane == j, 1.0, row) / pivot
            rest = jnp.where(lane == j, 0.0, panel) - column * scaled
            panel = jnp.where(sub == j, scaled, rest)
        whole = ref[...]
        updated = jnp.where(wide_lane < 8, 0.0, whole)
        for j in range(8):
            updated = updated - whole[:, j : j + 1] * panel[j : j + 1, :]
        ref[...] = pltpu.roll(updated, T - 8, 1)
        ref[pl.ds(start, 8), :] = pltpu.roll(panel, T - 8, 1)
        return carry

    lax.fori_loop(0, T // 8, step, 0)


def kernel(
    cls_ref, wave_ref, raw_hbm, data_hbm, rows_hbm, vals_hbm,
    raw, data, kk, rr, qq, mat, trow, dinv, cc, out, vals,
    load_sem, send_sem, recv_sem, store_sem,
):
    gx, gy = lax.axis_index("gx"), lax.axis_index("gy")
    size_x, size_y = lax.axis_size("gx"), lax.axis_size("gy")
    half_x, half_y = size_x // 2, size_y // 2
    col, row = gx // half_x, gy // half_y
    sib = (lax.rem(gx + half_x, size_x), gy)
    diag = (lax.rem(gx + half_x, size_x), lax.rem(gy + half_y, size_y))

    barrier = pltpu.get_barrier_semaphore()
    for peer in (sib, diag):
        pl.semaphore_signal(barrier, inc=1, device_id=peer, device_id_type=MESH)

    low, high = pl.ds(0, 384), pl.ds(384, 384)
    loads = []
    for i, (r, c) in enumerate(((high, high), (high, low), (low, high), (low, low))):
        copy = pltpu.make_async_copy(raw_hbm.at[r, c], raw.at[r, c], load_sem.at[i])
        copy.start()
        loads.append(copy)
    data_copy = pltpu.make_async_copy(data_hbm, data, load_sem.at[4])
    data_copy.start()

    OWN, SIB, DIA, OPP = 0, 1, 2, 3
    flow = [0]

    def send(src, dst, peer):
        i = flow[0]
        flow[0] += 1
        copy = pltpu.make_async_remote_copy(
            src_ref=src, dst_ref=dst, send_sem=send_sem.at[i], recv_sem=recv_sem.at[i],
            device_id=peer, device_id_type=MESH,
        )
        copy.start()
        return copy

    def krow(tile, i):
        return kk.at[tile, pl.ds(T * i, T), pl.ds(0, T * (i + 1))]

    def half(ref, tile, i):
        return ref.at[tile, pl.ds(192 * i, 192), :]

    iota_r = lax.broadcasted_iota(jnp.int32, (T, T), 0)
    iota_c = lax.broadcasted_iota(jnp.int32, (T, T), 1)

    def diagonal(block):
        first = 4.0 + wave_ref[cls_ref[2 * block]]
        second = 4.0 + wave_ref[cls_ref[2 * block + 1]]
        return jnp.where(iota_r == iota_c, jnp.where(iota_r < 64, first, second), 0.0)

    loads[0].wait()
    for i in range(3):
        for j in range(3):
            block = raw[pl.ds(384 + T * i, T), pl.ds(384 + T * j, T)]
            mirror = raw[pl.ds(384 + T * j, T), pl.ds(384 + T * i, T)]
            summed = 0.5 * (block + mirror.T)
            if i == j:
                summed = summed + diagonal(3 + i)
            kk[OWN, pl.ds(T * i, T), pl.ds(T * j, T)] = summed
    pl.semaphore_wait(barrier, 2)

    copies = []
    k_sib, k_dia = {}, {}
    for i in (2, 1, 0):
        k_sib[i] = send(krow(OWN, i), krow(SIB, i), sib)
    for i in (0, 1, 2):
        k_dia[i] = send(krow(OWN, i), krow(DIA, i), diag)

    loads[1].wait()
    loads[2].wait()
    for i in range(3):
        for j in range(3):
            block = raw[pl.ds(384 + T * i, T), pl.ds(T * j, T)]
            mirror = raw[pl.ds(T * j, T), pl.ds(384 + T * i, T)]
            rr[OWN, pl.ds(T * i, T), pl.ds(T * j, T)] = 0.5 * (block + mirror.T)
    data_copy.wait()
    qq[OWN] = product(rr[OWN], data[...])

    k_sib[2].wait_recv()
    k_opp = {2: send(krow(SIB, 2), krow(OPP, 2), diag)}
    for i in (0, 1):
        k_dia[i].wait_recv()
        k_opp[i] = send(krow(DIA, i), krow(OPP, i), sib)

    r_sib, r_dia, q_sib, q_dia = {}, {}, {}, {}
    for i in (0, 1):
        r_sib[i] = send(half(rr, OWN, i), half(rr, SIB, i), sib)
        r_dia[1 - i] = send(half(rr, OWN, 1 - i), half(rr, DIA, 1 - i), diag)
    for i in (0, 1):
        q_sib[i] = send(half(qq, OWN, i), half(qq, SIB, i), sib)
        q_dia[1 - i] = send(half(qq, OWN, 1 - i), half(qq, DIA, 1 - i), diag)

    k_sib[1].wait_recv()
    k_sib[0].wait_recv()
    k_dia[2].wait_recv()

    def tile_block(tile, i, j):
        if i >= j or tile == OWN:
            return kk[tile, pl.ds(T * i, T), pl.ds(T * j, T)]
        return kk[tile, pl.ds(T * j, T), pl.ds(T * i, T)].T

    for i in range(3):
        for j in range(3):
            row_y = iota_r + T * i < 192
            col_y = iota_c + T * j < 192
            own_block = tile_block(OWN, i, j)
            dia_block = tile_block(DIA, i, j)
            same = row_y == col_y
            yy = jnp.logical_and(row_y, col_y)
            yx = jnp.logical_and(row_y, jnp.logical_not(col_y))
            mat[j, pl.ds(T * i, T), :] = tile_block(SIB, i, j) + jnp.where(
                same, jnp.where(yy, dia_block, own_block), 0.0
            )
            mat[3 + j, pl.ds(384 + T * i, T), :] = jnp.where(
                same, jnp.where(yy, own_block, dia_block), 0.0
            )
            mat[3 + j, pl.ds(T * i, T), :] = jnp.where(
                same, 0.0, jnp.where(yx, dia_block, own_block)
            )
            mat[j, pl.ds(384 + T * i, T), :] = jnp.where(
                same, 0.0, jnp.where(yx, own_block, dia_block)
            )

    def sweep(b, carry):
        start = pl.multiple_of(b * T, T)
        dinv[...] = mat[b, pl.ds(start, T), :]
        invert_tile(dinv)
        inverse = dinv[...]

        def scale(j, c):
            trow[j] = product(inverse, mat[j, pl.ds(start, T), :])
            return c

        lax.fori_loop(0, 6, scale, 0)
        trow[b] = inverse
        column = mat[b]
        mat[b] = jnp.zeros((768, T), f32)

        def update(j, c):
            mat[j] = mat[j] - product(column, trow[j])
            mat[j, pl.ds(start, T), :] = trow[j]
            return c

        lax.fori_loop(0, 6, update, 0)
        return carry

    lax.fori_loop(0, 3, sweep, 0)
    for i in range(3):
        k_opp[i].wait_recv()
    for i in range(3):
        for j in range(3):
            mat[3 + j, pl.ds(384 + T * i, T), :] += tile_block(OPP, i, j)
    lax.fori_loop(3, 6, sweep, 0)

    r_sib[0].wait_recv()
    r_opp = {0: send(half(rr, SIB, 0), half(rr, OPP, 0), diag)}
    r_dia[1].wait_recv()
    r_opp[1] = send(half(rr, DIA, 1), half(rr, OPP, 1), sib)
    q_sib[0].wait_recv()
    q_opp = {0: send(half(qq, SIB, 0), half(qq, OPP, 0), diag)}
    q_dia[1].wait_recv()
    q_opp[1] = send(half(qq, DIA, 1), half(qq, OPP, 1), sib)

    own_rows = jnp.concatenate([rr[OWN, pl.ds(192, 192), :], rr[OWN, pl.ds(0, 192), :]], axis=0)
    for j in range(6):
        cc[j] = inner(own_rows, mat[j, pl.ds(192, 384), :])
    left = iota_c < 64
    left = lax.broadcasted_iota(jnp.int32, (384, T), 1) < 64

    def parts(tile):
        if tile == SIB:
            return cc[0], cc[1], cc[2]
        if tile == OPP:
            return cc[3], cc[4], cc[5]
        if tile == DIA:
            return cc[0], jnp.where(left, cc[1], cc[4]), cc[5]
        return cc[3], jnp.where(left, cc[4], cc[1]), cc[2]

    loads[3].wait()
    for i in range(3):
        for j in range(3):
            block = raw[pl.ds(T * i, T), pl.ds(T * j, T)]
            mirror = raw[pl.ds(T * j, T), pl.ds(T * i, T)]
            summed = 0.5 * (block + mirror.T)
            if i == j:
                summed = summed + diagonal(i)
            out[OWN, pl.ds(T * i, T), pl.ds(T * j, T)] = summed

    place = {
        OWN: 2 * row + col,
        SIB: 2 * row + 1 - col,
        DIA: 2 * (1 - row) + 1 - col,
        OPP: 2 * (1 - row) + col,
    }
    stores = []

    def finish(tile):
        total = None
        for j, part in enumerate(parts(tile)):
            term = product(part, rr[tile, pl.ds(T * j, T), :])
            total = term if total is None else total + term
        if tile == OWN:
            out[OWN] = out[OWN] - total
        else:
            out[tile] = -total
        copy = pltpu.make_async_copy(
            out.at[tile],
            rows_hbm.at[:, pl.ds(pl.multiple_of(place[tile] * 384, T), 384)],
            store_sem.at[tile],
        )
        copy.start()
        stores.append(copy)

    finish(OWN)
    r_sib[1].wait_recv()
    finish(SIB)
    r_dia[0].wait_recv()
    finish(DIA)
    r_opp[0].wait_recv()
    r_opp[1].wait_recv()
    finish(OPP)

    q_sib[1].wait_recv()
    q_dia[0].wait_recv()
    q_opp[0].wait_recv()
    q_opp[1].wait_recv()
    upper = lax.broadcasted_iota(jnp.int32, (384, T), 0) < 192
    first = qq[SIB] + jnp.where(upper, qq[DIA], qq[OWN])
    second = qq[OPP] + jnp.where(upper, qq[OWN], qq[DIA])
    total = None
    for j in range(6):
        side = first if j < 3 else second
        term = product(mat[j, pl.ds(192, 384), :], side[T * (j % 3) : T * (j % 3 + 1), :])
        total = term if total is None else total + term
    vals[pl.ds(0, 192), :] = -total[192:, :]
    vals[pl.ds(192, 192), :] = -total[:192, :]
    copy = pltpu.make_async_copy(vals, vals_hbm, store_sem.at[4])
    copy.start()
    stores.append(copy)

    for group in (k_sib, k_dia, k_opp, r_sib, r_dia, r_opp, q_sib, q_dia, q_opp):
        for i in group:
            group[i].wait_send()
    for copy in stores:
        copy.wait()


def body(leaf_raw, medium_class, wave_table, boundary_data):
    raw = leaf_raw[0, 0]
    data = boundary_data[0, 0]
    flows = 6 + 3 + 8 + 4
    rows, vals = pl.pallas_call(
        kernel,
        out_shape=(
            jax.ShapeDtypeStruct((384, 1536), f32),
            jax.ShapeDtypeStruct((384, T), f32),
        ),
        in_specs=[
            pl.BlockSpec(memory_space=pltpu.SMEM),
            pl.BlockSpec(memory_space=pltpu.SMEM),
            pl.BlockSpec(memory_space=pl.ANY),
            pl.BlockSpec(memory_space=pl.ANY),
        ],
        out_specs=(
            pl.BlockSpec(memory_space=pl.ANY),
            pl.BlockSpec(memory_space=pl.ANY),
        ),
        scratch_shapes=[
            pltpu.VMEM((768, 768), f32),
            pltpu.VMEM((384, T), f32),
            pltpu.VMEM((4, 384, 384), f32),
            pltpu.VMEM((4, 384, 384), f32),
            pltpu.VMEM((4, 384, T), f32),
            pltpu.VMEM((6, 768, T), f32),
            pltpu.VMEM((6, T, T), f32),
            pltpu.VMEM((T, T), f32),
            pltpu.VMEM((6, 384, T), f32),
            pltpu.VMEM((4, 384, 384), f32),
            pltpu.VMEM((384, T), f32),
            pltpu.SemaphoreType.DMA((5,)),
            pltpu.SemaphoreType.DMA((flows,)),
            pltpu.SemaphoreType.DMA((flows,)),
            pltpu.SemaphoreType.DMA((5,)),
        ],
        compiler_params=pltpu.CompilerParams(
            collective_id=0, has_side_effects=True, vmem_limit_bytes=48 << 20
        ),
    )(medium_class[0, 0], wave_table, raw, data)
    return rows[None, None], vals[None, None]


def solution(mesh):
    return jax.shard_map(
        body,
        mesh=mesh,
        in_specs=(P("gx", "gy", None, None), P("gx", "gy", None), P(), P("gx", "gy", None, None)),
        out_specs=(P("gx", "gy", None, None), P("gx", "gy", None, None)),
        check_vma=False,
    )
```

```python
import functools

import jax
import jax.numpy as jnp
from jax import lax
from jax.experimental import pallas as pl
from jax.experimental.pallas import tpu as pltpu
from jax.sharding import PartitionSpec as P

highest = lax.Precision.HIGHEST
MESH = pl.DeviceIdType.MESH
T = 128
PANEL = 16
SHARE = 32
f32 = jnp.float32


def product(left, right):
    return jnp.dot(left, right, precision=highest, preferred_element_type=f32)


def inner(left, right):
    return lax.dot_general(
        left, right, (((0,), (0,)), ((), ())), precision=highest, preferred_element_type=f32
    )


def invert_tile(ref):
    lane = lax.broadcasted_iota(jnp.int32, (PANEL, T), 1)
    sub = lax.broadcasted_iota(jnp.int32, (PANEL, T), 0)
    wide_lane = lax.broadcasted_iota(jnp.int32, (T, T), 1)

    def spread(block, j):
        return jnp.broadcast_to(block[j : j + 1, :], (PANEL, T))

    def step(k, carry):
        start = pl.multiple_of(k * PANEL, PANEL)
        panel = ref[pl.ds(start, PANEL), :]
        whole = ref[...]
        columns = [jnp.broadcast_to(panel[:, m : m + 1], (PANEL, T)) for m in range(PANEL)]
        for j in range(PANEL):
            column = columns[j]
            inverse = 1.0 / spread(column, j)
            scaled = jnp.where(lane == j, inverse, spread(panel, j) * inverse)
            rest = jnp.where(lane == j, 0.0, panel) - column * scaled
            panel = jnp.where(sub == j, scaled, rest)
            for m in range(j + 1, PANEL):
                pivot_row = spread(columns[m], j) * inverse
                columns[m] = jnp.where(sub == j, pivot_row, columns[m] - column * pivot_row)
        updated = jnp.where(wide_lane < PANEL, 0.0, whole)
        for j in range(PANEL):
            updated = updated - whole[:, j : j + 1] * panel[j : j + 1, :]
        ref[...] = pltpu.roll(updated, T - PANEL, 1)
        ref[pl.ds(start, PANEL), :] = pltpu.roll(panel, T - PANEL, 1)
        return carry

    lax.fori_loop(0, T // PANEL, step, 0)


def kernel(
    cls_ref, wave_ref, raw_hbm, data_hbm, rows_hbm, vals_hbm,
    raw, data, pk, kk, rr, qt, qin, mat, trow, dinv, cc, out, vt, vin, vals,
    load_sem, send_sem, recv_sem, store_sem,
):
    gx, gy = lax.axis_index("gx"), lax.axis_index("gy")
    size_x, size_y = lax.axis_size("gx"), lax.axis_size("gy")
    half_x, half_y = size_x // 2, size_y // 2
    col, row = gx // half_x, gy // half_y
    other_x, other_y = lax.rem(gx + half_x, size_x), lax.rem(gy + half_y, size_y)
    sib, diag, opp = (other_x, gy), (other_x, other_y), (gx, other_y)

    barrier = pltpu.get_barrier_semaphore()
    for peer in (sib, diag, opp):
        pl.semaphore_signal(barrier, inc=1, device_id=peer, device_id_type=MESH)

    low, high = pl.ds(0, 384), pl.ds(384, 384)
    loads = []
    for i, (r, c) in enumerate(((high, high), (high, low), (low, high), (low, low))):
        copy = pltpu.make_async_copy(raw_hbm.at[r, c], raw.at[r, c], load_sem.at[i])
        copy.start()
        loads.append(copy)
    data_copy = pltpu.make_async_copy(data_hbm, data, load_sem.at[4])
    data_copy.start()

    OWN, SIB, DIA, OPP = 0, 1, 2, 3
    place = {
        OWN: 2 * row + col,
        SIB: 2 * row + 1 - col,
        DIA: 2 * (1 - row) + 1 - col,
        OPP: 2 * (1 - row) + col,
    }
    flow = [0]
    sent = []

    def send(src, dst, peer):
        i = flow[0]
        flow[0] += 1
        copy = pltpu.make_async_remote_copy(
            src_ref=src, dst_ref=dst, send_sem=send_sem.at[i], recv_sem=recv_sem.at[i],
            device_id=peer, device_id_type=MESH,
        )
        copy.start()
        sent.append(copy)
        return copy

    def share(tile):
        return pl.ds(pl.multiple_of(place[tile] * SHARE, SHARE), SHARE)

    def khalf(tile, i):
        return pk.at[tile, pl.ds(0, 104) if i == 0 else pl.ds(104, 96), :]

    def rhalf(tile, i):
        return rr.at[tile, pl.ds(192 * i, 192), :]

    iota_r = lax.broadcasted_iota(jnp.int32, (T, T), 0)
    iota_c = lax.broadcasted_iota(jnp.int32, (T, T), 1)
    long_r = lax.broadcasted_iota(jnp.int32, (192, 384), 0)
    long_c = lax.broadcasted_iota(jnp.int32, (192, 384), 1)

    def diagonal(block):
        first = 4.0 + wave_ref[cls_ref[2 * block]]
        second = 4.0 + wave_ref[cls_ref[2 * block + 1]]
        return jnp.where(iota_r == iota_c, jnp.where(iota_r < 64, first, second), 0.0)

    loads[0].wait()
    for i in range(3):
        for j in range(3):
            block = raw[pl.ds(384 + T * i, T), pl.ds(384 + T * j, T)]
            mirror = raw[pl.ds(384 + T * j, T), pl.ds(384 + T * i, T)]
            summed = 0.5 * (block + mirror.T)
            if i == j:
                summed = summed + diagonal(3 + i)
            kk[OWN, pl.ds(T * i, T), pl.ds(T * j, T)] = summed

    shifted = pltpu.roll(kk[OWN, pl.ds(192, 192), :], 192, 1)
    in_y = long_c < 192
    pk[OWN, pl.ds(0, 192), :] = jnp.where(
        jnp.logical_and(in_y, long_c > long_r), shifted, kk[OWN, pl.ds(0, 192), :]
    )
    main = jnp.sum(jnp.where(long_c == long_r, shifted, 0.0), axis=0, keepdims=True)
    pk[OWN, pl.ds(192, 8), :] = jnp.broadcast_to(main, (8, 384))
    pl.semaphore_wait(barrier, 3)

    k_sib, k_dia = {}, {}
    for i in (0, 1):
        k_sib[i] = send(khalf(OWN, i), khalf(SIB, i), sib)
        k_dia[1 - i] = send(khalf(OWN, 1 - i), khalf(DIA, 1 - i), diag)

    loads[1].wait()
    loads[2].wait()
    for i in range(3):
        for j in range(3):
            block = raw[pl.ds(384 + T * i, T), pl.ds(T * j, T)]
            mirror = raw[pl.ds(T * j, T), pl.ds(384 + T * i, T)]
            rr[OWN, pl.ds(T * i, T), pl.ds(T * j, T)] = 0.5 * (block + mirror.T)
    data_copy.wait()
    qt[...] = lax.dot_general(
        data[...].T, rr[OWN], (((1,), (1,)), ((), ())),
        precision=highest, preferred_element_type=f32,
    )

    k_sib[0].wait_recv()
    k_opp = {0: send(khalf(SIB, 0), khalf(OPP, 0), diag)}
    k_dia[1].wait_recv()
    k_opp[1] = send(khalf(DIA, 1), khalf(OPP, 1), sib)

    q_in = [
        send(qt.at[share(OPP), :], qin.at[OPP], opp),
        send(qt.at[share(SIB), :], qin.at[SIB], sib),
        send(qt.at[share(DIA), :], qin.at[DIA], diag),
    ]
    r_sib, r_dia = {}, {}
    for i in (0, 1):
        r_sib[i] = send(rhalf(OWN, i), rhalf(SIB, i), sib)
        r_dia[1 - i] = send(rhalf(OWN, 1 - i), rhalf(DIA, 1 - i), diag)

    def unpack(tile):
        packed = pk[tile, pl.ds(0, 192), :]
        padded = jnp.concatenate([packed[T:, :], jnp.zeros((64, 384), f32)], axis=0)
        turned = []
        for i in range(3):
            lanes = slice(T * i, T * (i + 1))
            turned.append(
                jnp.concatenate(
                    [packed[:T, lanes].T, padded[:, lanes].T, jnp.zeros((T, T), f32)], axis=1
                )
            )
        turned = jnp.concatenate(turned, axis=0)
        top, bottom = turned[:192, :], turned[192:, :]
        kk[tile, pl.ds(0, 192), :] = jnp.where(
            jnp.logical_or(long_c >= 192, long_r >= long_c), packed, top
        )
        xx = jnp.where(
            long_r == long_c,
            jnp.broadcast_to(pk[tile, pl.ds(192, 1), :], (192, 384)),
            jnp.where(long_c > long_r, packed, top),
        )
        kk[tile, pl.ds(192, 192), :] = jnp.where(in_y, bottom, pltpu.roll(xx, 192, 1))

    def kblock(tile, i, j):
        return kk[tile, pl.ds(T * i, T), pl.ds(T * j, T)]

    k_sib[1].wait_recv()
    unpack(SIB)
    k_dia[0].wait_recv()
    unpack(DIA)
    for i in range(3):
        for j in range(3):
            row_y = iota_r + T * i < 192
            col_y = iota_c + T * j < 192
            own_block = kblock(OWN, i, j)
            dia_block = kblock(DIA, i, j)
            same = row_y == col_y
            yy = jnp.logical_and(row_y, col_y)
            yx = jnp.logical_and(row_y, jnp.logical_not(col_y))
            mat[j, pl.ds(T * i, T), :] = kblock(SIB, i, j) + jnp.where(
                same, jnp.where(yy, dia_block, own_block), 0.0
            )
            mat[3 + j, pl.ds(384 + T * i, T), :] = jnp.where(
                same, jnp.where(yy, own_block, dia_block), 0.0
            )
            mat[3 + j, pl.ds(T * i, T), :] = jnp.where(
                same, 0.0, jnp.where(yx, dia_block, own_block)
            )
            mat[j, pl.ds(384 + T * i, T), :] = jnp.where(
                same, 0.0, jnp.where(yx, own_block, dia_block)
            )

    def sweep(b, carry):
        start = pl.multiple_of(b * T, T)
        dinv[...] = mat[b, pl.ds(start, T), :]
        invert_tile(dinv)
        inverse = dinv[...]
        for j in range(6):
            trow[j] = product(inverse, mat[j, pl.ds(start, T), :])
        trow[b] = inverse
        column = mat[b]
        mat[b] = jnp.zeros((768, T), f32)
        for j in range(6):
            mat[j] = mat[j] - product(column, trow[j])
            mat[j, pl.ds(start, T), :] = trow[j]
        return carry

    lax.fori_loop(0, 3, sweep, 0)
    for i in range(2):
        k_opp[i].wait_recv()
    unpack(OPP)
    for i in range(3):
        for j in range(3):
            mat[3 + j, pl.ds(384 + T * i, T), :] += kblock(OPP, i, j)
    lax.fori_loop(3, 6, sweep, 0)

    for copy in q_in:
        copy.wait_recv()
    wide = lax.broadcasted_iota(jnp.int32, (SHARE, 384), 1) < 192
    own_q = qt[share(OWN), :]
    first = qin[SIB] + jnp.where(wide, qin[DIA], own_q)
    second = qin[OPP] + jnp.where(wide, own_q, qin[DIA])
    sides = jnp.concatenate([first, second], axis=1)
    solved = [-product(sides, mat[j]) for j in range(6)]
    near = jnp.concatenate(solved[:3], axis=1)
    far = jnp.concatenate(solved[3:], axis=1)
    vt[SIB] = near
    vt[OPP] = far
    vt[DIA] = jnp.where(wide, near, far)
    vin[share(OWN), :] = jnp.where(wide, far, near)

    r_sib[0].wait_recv()
    r_opp = {0: send(rhalf(SIB, 0), rhalf(OPP, 0), diag)}
    r_dia[1].wait_recv()
    r_opp[1] = send(rhalf(DIA, 1), rhalf(OPP, 1), sib)
    v_in = [
        send(vt.at[OPP], vin.at[share(OWN), :], opp),
        send(vt.at[SIB], vin.at[share(OWN), :], sib),
        send(vt.at[DIA], vin.at[share(OWN), :], diag),
    ]

    own_rows = jnp.concatenate([rr[OWN, pl.ds(192, 192), :], rr[OWN, pl.ds(0, 192), :]], axis=0)
    for j in range(6):
        cc[j] = inner(own_rows, mat[j, pl.ds(192, 384), :])
    left = lax.broadcasted_iota(jnp.int32, (384, T), 1) < 64

    def parts(tile):
        if tile == SIB:
            return cc[0], cc[1], cc[2]
        if tile == OPP:
            return cc[3], cc[4], cc[5]
        if tile == DIA:
            return cc[0], jnp.where(left, cc[1], cc[4]), cc[5]
        return cc[3], jnp.where(left, cc[4], cc[1]), cc[2]

    loads[3].wait()
    for i in range(3):
        for j in range(3):
            block = raw[pl.ds(T * i, T), pl.ds(T * j, T)]
            mirror = raw[pl.ds(T * j, T), pl.ds(T * i, T)]
            summed = 0.5 * (block + mirror.T)
            if i == j:
                summed = summed + diagonal(i)
            out[OWN, pl.ds(T * i, T), pl.ds(T * j, T)] = summed

    stores = []

    def finish(tile):
        total = None
        for j, part in enumerate(parts(tile)):
            term = product(part, rr[tile, pl.ds(T * j, T), :])
            total = term if total is None else total + term
        if tile == OWN:
            out[OWN] = out[OWN] - total
        else:
            out[tile] = -total
        copy = pltpu.make_async_copy(
            out.at[tile],
            rows_hbm.at[:, pl.ds(pl.multiple_of(place[tile] * 384, T), 384)],
            store_sem.at[tile],
        )
        copy.start()
        stores.append(copy)

    finish(OWN)
    r_sib[1].wait_recv()
    finish(SIB)
    r_dia[0].wait_recv()
    finish(DIA)
    r_opp[0].wait_recv()
    r_opp[1].wait_recv()
    finish(OPP)

    for copy in v_in:
        copy.wait_recv()
    vals[...] = vin[...].T
    copy = pltpu.make_async_copy(vals, vals_hbm, store_sem.at[4])
    copy.start()
    stores.append(copy)

    for copy in sent:
        copy.wait_send()
    for copy in stores:
        copy.wait()


def body(leaf_raw, medium_class, wave_table, boundary_data):
    raw = leaf_raw[0, 0]
    data = boundary_data[0, 0]
    flows = 18
    rows, vals = pl.pallas_call(
        kernel,
        out_shape=(
            jax.ShapeDtypeStruct((384, 1536), f32),
            jax.ShapeDtypeStruct((384, T), f32),
        ),
        in_specs=[
            pl.BlockSpec(memory_space=pltpu.SMEM),
            pl.BlockSpec(memory_space=pltpu.SMEM),
            pl.BlockSpec(memory_space=pl.ANY),
            pl.BlockSpec(memory_space=pl.ANY),
        ],
        out_specs=(
            pl.BlockSpec(memory_space=pl.ANY),
            pl.BlockSpec(memory_space=pl.ANY),
        ),
        scratch_shapes=[
            pltpu.VMEM((768, 768), f32),
            pltpu.VMEM((384, T), f32),
            pltpu.VMEM((4, 200, 384), f32),
            pltpu.VMEM((4, 384, 384), f32),
            pltpu.VMEM((4, 384, 384), f32),
            pltpu.VMEM((T, 384), f32),
            pltpu.VMEM((4, SHARE, 384), f32),
            pltpu.VMEM((6, 768, T), f32),
            pltpu.VMEM((6, T, T), f32),
            pltpu.VMEM((T, T), f32),
            pltpu.VMEM((6, 384, T), f32),
            pltpu.VMEM((4, 384, 384), f32),
            pltpu.VMEM((4, SHARE, 384), f32),
            pltpu.VMEM((T, 384), f32),
            pltpu.VMEM((384, T), f32),
            pltpu.SemaphoreType.DMA((5,)),
            pltpu.SemaphoreType.DMA((flows,)),
            pltpu.SemaphoreType.DMA((flows,)),
            pltpu.SemaphoreType.DMA((5,)),
        ],
        compiler_params=pltpu.CompilerParams(
            collective_id=0, has_side_effects=True, vmem_limit_bytes=66 * 1000 * 1000
        ),
    )(medium_class[0, 0], wave_table, raw, data)
    return rows[None, None], vals[None, None]


def solution(mesh):
    return jax.shard_map(
        body,
        mesh=mesh,
        in_specs=(P("gx", "gy", None, None), P("gx", "gy", None), P(), P("gx", "gy", None, None)),
        out_specs=(P("gx", "gy", None, None), P("gx", "gy", None, None)),
        check_vma=False,
    )
```

```python
import functools

import jax
import jax.numpy as jnp
from jax import lax
from jax.experimental import pallas as pl
from jax.experimental.pallas import tpu as pltpu
from jax.sharding import PartitionSpec as P

highest = lax.Precision.HIGHEST
MESH = pl.DeviceIdType.MESH
T = 128
PANEL = 16
SHARE = 32
f32 = jnp.float32


def product(left, right):
    return jnp.dot(left, right, precision=highest, preferred_element_type=f32)


def inner(left, right):
    return lax.dot_general(
        left, right, (((0,), (0,)), ((), ())), precision=highest, preferred_element_type=f32
    )


def invert_tile(ref):
    lane = lax.broadcasted_iota(jnp.int32, (PANEL, T), 1)
    sub = lax.broadcasted_iota(jnp.int32, (PANEL, T), 0)
    wide_lane = lax.broadcasted_iota(jnp.int32, (T, T), 1)

    def spread(block, j):
        return jnp.broadcast_to(block[j : j + 1, :], (PANEL, T))

    def step(k, carry):
        start = pl.multiple_of(k * PANEL, PANEL)
        panel = ref[pl.ds(start, PANEL), :]
        whole = ref[...]
        columns = [jnp.broadcast_to(panel[:, m : m + 1], (PANEL, T)) for m in range(PANEL)]
        for j in range(PANEL):
            column = columns[j]
            inverse = 1.0 / spread(column, j)
            scaled = jnp.where(lane == j, inverse, spread(panel, j) * inverse)
            rest = jnp.where(lane == j, 0.0, panel) - column * scaled
            panel = jnp.where(sub == j, scaled, rest)
            for m in range(j + 1, PANEL):
                pivot_row = spread(columns[m], j) * inverse
                columns[m] = jnp.where(sub == j, pivot_row, columns[m] - column * pivot_row)
        updated = jnp.where(wide_lane < PANEL, 0.0, whole)
        for j in range(PANEL):
            updated = updated - whole[:, j : j + 1] * panel[j : j + 1, :]
        ref[...] = pltpu.roll(updated, T - PANEL, 1)
        ref[pl.ds(start, PANEL), :] = pltpu.roll(panel, T - PANEL, 1)
        return carry

    lax.fori_loop(0, T // PANEL, step, 0)


def kernel(
    cls_ref, wave_ref, raw_hbm, data_hbm, rows_hbm, vals_hbm,
    raw, data, pk, kk, rr, qt, qin, mat, trow, dinv, cc, out, vt, vin, vals,
    load_sem, send_sem, recv_sem, store_sem,
):
    gx, gy = lax.axis_index("gx"), lax.axis_index("gy")
    size_x, size_y = lax.axis_size("gx"), lax.axis_size("gy")
    half_x, half_y = size_x // 2, size_y // 2
    col, row = gx // half_x, gy // half_y
    other_x, other_y = lax.rem(gx + half_x, size_x), lax.rem(gy + half_y, size_y)
    sib, diag, opp = (other_x, gy), (other_x, other_y), (gx, other_y)

    barrier = pltpu.get_barrier_semaphore()
    for peer in (sib, diag, opp):
        pl.semaphore_signal(barrier, inc=1, device_id=peer, device_id_type=MESH)

    low, high = pl.ds(0, 384), pl.ds(384, 384)
    loads = []
    for i, (r, c) in enumerate(((high, high), (high, low), (low, high), (low, low))):
        copy = pltpu.make_async_copy(raw_hbm.at[r, c], raw.at[r, c], load_sem.at[i])
        copy.start()
        loads.append(copy)
    data_copy = pltpu.make_async_copy(data_hbm, data, load_sem.at[4])
    data_copy.start()

    OWN, SIB, DIA, OPP = 0, 1, 2, 3
    place = {
        OWN: 2 * row + col,
        SIB: 2 * row + 1 - col,
        DIA: 2 * (1 - row) + 1 - col,
        OPP: 2 * (1 - row) + col,
    }
    flow = [0]
    sent = []

    def send(src, dst, peer):
        i = flow[0]
        flow[0] += 1
        copy = pltpu.make_async_remote_copy(
            src_ref=src, dst_ref=dst, send_sem=send_sem.at[i], recv_sem=recv_sem.at[i],
            device_id=peer, device_id_type=MESH,
        )
        copy.start()
        sent.append(copy)
        return copy

    def share(tile):
        return pl.ds(pl.multiple_of(place[tile] * SHARE, SHARE), SHARE)

    def khalf(tile, i):
        return pk.at[tile, pl.ds(0, 104) if i == 0 else pl.ds(104, 96), :]

    def rchunk(tile, start, size):
        return rr.at[tile, pl.ds(start, size), :]

    iota_r = lax.broadcasted_iota(jnp.int32, (T, T), 0)
    iota_c = lax.broadcasted_iota(jnp.int32, (T, T), 1)
    long_r = lax.broadcasted_iota(jnp.int32, (192, 384), 0)
    long_c = lax.broadcasted_iota(jnp.int32, (192, 384), 1)

    def diagonal(block):
        first = 4.0 + wave_ref[cls_ref[2 * block]]
        second = 4.0 + wave_ref[cls_ref[2 * block + 1]]
        return jnp.where(iota_r == iota_c, jnp.where(iota_r < 64, first, second), 0.0)

    loads[0].wait()
    for i in range(3):
        for j in range(3):
            block = raw[pl.ds(384 + T * i, T), pl.ds(384 + T * j, T)]
            mirror = raw[pl.ds(384 + T * j, T), pl.ds(384 + T * i, T)]
            summed = 0.5 * (block + mirror.T)
            if i == j:
                summed = summed + diagonal(3 + i)
            kk[OWN, pl.ds(T * i, T), pl.ds(T * j, T)] = summed

    shifted = pltpu.roll(kk[OWN, pl.ds(192, 192), :], 192, 1)
    in_y = long_c < 192
    pk[OWN, pl.ds(0, 192), :] = jnp.where(
        jnp.logical_and(in_y, long_c > long_r), shifted, kk[OWN, pl.ds(0, 192), :]
    )
    main = jnp.sum(jnp.where(long_c == long_r, shifted, 0.0), axis=0, keepdims=True)
    pk[OWN, pl.ds(192, 8), :] = jnp.broadcast_to(main, (8, 384))
    pl.semaphore_wait(barrier, 3)

    k_sib, k_dia = {}, {}
    for i in (0, 1):
        k_sib[i] = send(khalf(OWN, i), khalf(SIB, i), sib)
        k_dia[1 - i] = send(khalf(OWN, 1 - i), khalf(DIA, 1 - i), diag)

    loads[1].wait()
    loads[2].wait()
    for i in range(3):
        for j in range(3):
            block = raw[pl.ds(384 + T * i, T), pl.ds(T * j, T)]
            mirror = raw[pl.ds(T * j, T), pl.ds(384 + T * i, T)]
            rr[OWN, pl.ds(T * i, T), pl.ds(T * j, T)] = 0.5 * (block + mirror.T)
    data_copy.wait()
    qt[...] = lax.dot_general(
        data[...].T, rr[OWN], (((1,), (1,)), ((), ())),
        precision=highest, preferred_element_type=f32,
    )

    k_sib[0].wait_recv()
    k_opp = {0: send(khalf(SIB, 0), khalf(OPP, 0), diag)}
    k_dia[1].wait_recv()
    k_opp[1] = send(khalf(DIA, 1), khalf(OPP, 1), sib)

    q_in = [
        send(qt.at[share(OPP), :], qin.at[OPP], opp),
        send(qt.at[share(SIB), :], qin.at[SIB], sib),
        send(qt.at[share(DIA), :], qin.at[DIA], diag),
    ]

    def send_rows(start, size, peer, tile):
        return send(rchunk(OWN, start, size), rchunk(tile, start, size), peer)

    r_sib = [send_rows(0, T, sib, SIB)]
    r_dia = [send_rows(256, T, diag, DIA)]
    r_sib += [send_rows(T, 64, sib, SIB), send_rows(192, 192, sib, SIB)]
    r_dia += [send_rows(192, 64, diag, DIA), send_rows(0, 192, diag, DIA)]

    def unpack(tile):
        packed = pk[tile, pl.ds(0, 192), :]
        padded = jnp.concatenate([packed[T:, :], jnp.zeros((64, 384), f32)], axis=0)
        turned = []
        for i in range(3):
            lanes = slice(T * i, T * (i + 1))
            turned.append(
                jnp.concatenate(
                    [packed[:T, lanes].T, padded[:, lanes].T, jnp.zeros((T, T), f32)], axis=1
                )
            )
        turned = jnp.concatenate(turned, axis=0)
        top, bottom = turned[:192, :], turned[192:, :]
        kk[tile, pl.ds(0, 192), :] = jnp.where(
            jnp.logical_or(long_c >= 192, long_r >= long_c), packed, top
        )
        xx = jnp.where(
            long_r == long_c,
            jnp.broadcast_to(pk[tile, pl.ds(192, 1), :], (192, 384)),
            jnp.where(long_c > long_r, packed, top),
        )
        kk[tile, pl.ds(192, 192), :] = jnp.where(in_y, bottom, pltpu.roll(xx, 192, 1))

    def kblock(tile, i, j):
        return kk[tile, pl.ds(T * i, T), pl.ds(T * j, T)]

    k_sib[1].wait_recv()
    unpack(SIB)
    k_dia[0].wait_recv()
    unpack(DIA)
    for i in range(3):
        for j in range(3):
            row_y = iota_r + T * i < 192
            col_y = iota_c + T * j < 192
            own_block = kblock(OWN, i, j)
            dia_block = kblock(DIA, i, j)
            same = row_y == col_y
            yy = jnp.logical_and(row_y, col_y)
            yx = jnp.logical_and(row_y, jnp.logical_not(col_y))
            mat[j, pl.ds(T * i, T), :] = kblock(SIB, i, j) + jnp.where(
                same, jnp.where(yy, dia_block, own_block), 0.0
            )
            mat[3 + j, pl.ds(384 + T * i, T), :] = jnp.where(
                same, jnp.where(yy, own_block, dia_block), 0.0
            )
            mat[3 + j, pl.ds(T * i, T), :] = jnp.where(
                same, 0.0, jnp.where(yx, dia_block, own_block)
            )
            mat[j, pl.ds(384 + T * i, T), :] = jnp.where(
                same, 0.0, jnp.where(yx, own_block, dia_block)
            )

    def sweep(b, carry):
        start = pl.multiple_of(b * T, T)
        dinv[...] = mat[b, pl.ds(start, T), :]
        invert_tile(dinv)
        inverse = dinv[...]
        for j in range(6):
            trow[j] = product(inverse, mat[j, pl.ds(start, T), :])
        trow[b] = inverse
        column = mat[b]
        mat[b] = jnp.zeros((768, T), f32)
        for j in range(6):
            mat[j] = mat[j] - product(column, trow[j])
            mat[j, pl.ds(start, T), :] = trow[j]
        return carry

    lax.fori_loop(0, 3, sweep, 0)
    for i in range(2):
        k_opp[i].wait_recv()
    unpack(OPP)
    for i in range(3):
        for j in range(3):
            mat[3 + j, pl.ds(384 + T * i, T), :] += kblock(OPP, i, j)
    lax.fori_loop(3, 6, sweep, 0)


    for copy in q_in:
        copy.wait_recv()
    wide = lax.broadcasted_iota(jnp.int32, (SHARE, 384), 1) < 192
    own_q = qt[share(OWN), :]
    first = qin[SIB] + jnp.where(wide, qin[DIA], own_q)
    second = qin[OPP] + jnp.where(wide, own_q, qin[DIA])
    sides = jnp.concatenate([first, second], axis=1)
    solved = [-product(sides, mat[j]) for j in range(6)]
    near = jnp.concatenate(solved[:3], axis=1)
    far = jnp.concatenate(solved[3:], axis=1)
    vt[SIB] = near
    vt[OPP] = far
    vt[DIA] = jnp.where(wide, near, far)
    vin[share(OWN), :] = jnp.where(wide, far, near)

    v_in = [
        send(vt.at[OPP], vin.at[share(OWN), :], opp),
        send(vt.at[SIB], vin.at[share(OWN), :], sib),
        send(vt.at[DIA], vin.at[share(OWN), :], diag),
    ]
    r_opp = []
    r_sib[0].wait_recv()
    r_opp.append(send(rchunk(SIB, 0, T), rchunk(OPP, 0, T), diag))
    r_dia[0].wait_recv()
    r_opp.append(send(rchunk(DIA, 256, T), rchunk(OPP, 256, T), sib))
    r_sib[1].wait_recv()
    r_opp.append(send(rchunk(SIB, T, 64), rchunk(OPP, T, 64), diag))
    r_dia[1].wait_recv()
    r_opp.append(send(rchunk(DIA, 192, 64), rchunk(OPP, 192, 64), sib))

    own_rows = jnp.concatenate([rr[OWN, pl.ds(192, 192), :], rr[OWN, pl.ds(0, 192), :]], axis=0)
    for j in range(6):
        cc[j] = inner(own_rows, mat[j, pl.ds(192, 384), :])
    left = lax.broadcasted_iota(jnp.int32, (384, T), 1) < 64

    def parts(tile):
        if tile == SIB:
            return cc[0], cc[1], cc[2]
        if tile == OPP:
            return cc[3], cc[4], cc[5]
        if tile == DIA:
            return cc[0], jnp.where(left, cc[1], cc[4]), cc[5]
        return cc[3], jnp.where(left, cc[4], cc[1]), cc[2]

    loads[3].wait()
    for i in range(3):
        for j in range(3):
            block = raw[pl.ds(T * i, T), pl.ds(T * j, T)]
            mirror = raw[pl.ds(T * j, T), pl.ds(T * i, T)]
            summed = 0.5 * (block + mirror.T)
            if i == j:
                summed = summed + diagonal(i)
            out[OWN, pl.ds(T * i, T), pl.ds(T * j, T)] = summed

    stores = []

    def term(tile, j):
        return product(parts(tile)[j], rr[tile, pl.ds(T * j, T), :])

    def store(tile):
        copy = pltpu.make_async_copy(
            out.at[tile],
            rows_hbm.at[:, pl.ds(pl.multiple_of(place[tile] * 384, T), 384)],
            store_sem.at[tile],
        )
        copy.start()
        stores.append(copy)

    out[OWN] = out[OWN] - (term(OWN, 0) + term(OWN, 1) + term(OWN, 2))
    store(OWN)
    r_sib[2].wait_recv()
    out[SIB] = -(term(SIB, 0) + term(SIB, 1) + term(SIB, 2))
    store(SIB)
    r_dia[2].wait_recv()
    out[DIA] = -(term(DIA, 0) + term(DIA, 1) + term(DIA, 2))
    store(DIA)
    r_opp[0].wait_recv()
    r_opp[1].wait_recv()
    out[OPP] = -(term(OPP, 0) + term(OPP, 2))
    for copy in v_in:
        copy.wait_recv()
    vals[...] = vin[...].T
    copy = pltpu.make_async_copy(vals, vals_hbm, store_sem.at[4])
    copy.start()
    stores.append(copy)

    r_opp[2].wait_recv()
    r_opp[3].wait_recv()
    out[OPP] = out[OPP] - term(OPP, 1)
    store(OPP)

    for copy in sent:
        copy.wait_send()
    for copy in stores:
        copy.wait()


def body(leaf_raw, medium_class, wave_table, boundary_data):
    raw = leaf_raw[0, 0]
    data = boundary_data[0, 0]
    flows = 22
    rows, vals = pl.pallas_call(
        kernel,
        out_shape=(
            jax.ShapeDtypeStruct((384, 1536), f32),
            jax.ShapeDtypeStruct((384, T), f32),
        ),
        in_specs=[
            pl.BlockSpec(memory_space=pltpu.SMEM),
            pl.BlockSpec(memory_space=pltpu.SMEM),
            pl.BlockSpec(memory_space=pltpu.HBM),
            pl.BlockSpec(memory_space=pltpu.HBM),
        ],
        out_specs=(
            pl.BlockSpec(memory_space=pl.ANY),
            pl.BlockSpec(memory_space=pl.ANY),
        ),
        scratch_shapes=[
            pltpu.VMEM((768, 768), f32),
            pltpu.VMEM((384, T), f32),
            pltpu.VMEM((4, 200, 384), f32),
            pltpu.VMEM((4, 384, 384), f32),
            pltpu.VMEM((4, 384, 384), f32),
            pltpu.VMEM((T, 384), f32),
            pltpu.VMEM((4, SHARE, 384), f32),
            pltpu.VMEM((6, 768, T), f32),
            pltpu.VMEM((6, T, T), f32),
            pltpu.VMEM((T, T), f32),
            pltpu.VMEM((6, 384, T), f32),
            pltpu.VMEM((4, 384, 384), f32),
            pltpu.VMEM((4, SHARE, 384), f32),
            pltpu.VMEM((T, 384), f32),
            pltpu.VMEM((384, T), f32),
            pltpu.SemaphoreType.DMA((5,)),
            pltpu.SemaphoreType.DMA((flows,)),
            pltpu.SemaphoreType.DMA((flows,)),
            pltpu.SemaphoreType.DMA((5,)),
        ],
        compiler_params=pltpu.CompilerParams(
            collective_id=0, has_side_effects=True, vmem_limit_bytes=48 << 20
        ),
    )(medium_class[0, 0], wave_table, raw, data)
    return rows[None, None], vals[None, None]


def solution(mesh):
    return jax.shard_map(
        body,
        mesh=mesh,
        in_specs=(P("gx", "gy", None, None), P("gx", "gy", None), P(), P("gx", "gy", None, None)),
        out_specs=(P("gx", "gy", None, None), P("gx", "gy", None, None)),
        check_vma=False,
    )
```

```python
import functools

import jax
import jax.numpy as jnp
from jax import lax
from jax.experimental import pallas as pl
from jax.experimental.pallas import tpu as pltpu
from jax.sharding import PartitionSpec as P

highest = lax.Precision.HIGHEST
MESH = pl.DeviceIdType.MESH
T = 128
PANEL = 16
SHARE = 32
f32 = jnp.float32


def product(left, right):
    return jnp.dot(left, right, precision=highest, preferred_element_type=f32)


def inner(left, right):
    return lax.dot_general(
        left, right, (((0,), (0,)), ((), ())), precision=highest, preferred_element_type=f32
    )


def invert_tile(ref):
    lane = lax.broadcasted_iota(jnp.int32, (PANEL, T), 1)
    sub = lax.broadcasted_iota(jnp.int32, (PANEL, T), 0)
    wide_lane = lax.broadcasted_iota(jnp.int32, (T, T), 1)

    def spread(block, j):
        return jnp.broadcast_to(block[j : j + 1, :], (PANEL, T))

    def step(k, carry):
        start = pl.multiple_of(k * PANEL, PANEL)
        panel = ref[pl.ds(start, PANEL), :]
        whole = ref[...]
        columns = [jnp.broadcast_to(panel[:, m : m + 1], (PANEL, T)) for m in range(PANEL)]
        for j in range(PANEL):
            column = columns[j]
            inverse = 1.0 / spread(column, j)
            scaled = jnp.where(lane == j, inverse, spread(panel, j) * inverse)
            rest = jnp.where(lane == j, 0.0, panel) - column * scaled
            panel = jnp.where(sub == j, scaled, rest)
            for m in range(j + 1, PANEL):
                pivot_row = spread(columns[m], j) * inverse
                columns[m] = jnp.where(sub == j, pivot_row, columns[m] - column * pivot_row)
        updated = jnp.where(wide_lane < PANEL, 0.0, whole)
        for j in range(PANEL):
            updated = updated - whole[:, j : j + 1] * panel[j : j + 1, :]
        ref[...] = pltpu.roll(updated, T - PANEL, 1)
        ref[pl.ds(start, PANEL), :] = pltpu.roll(panel, T - PANEL, 1)
        return carry

    lax.fori_loop(0, T // PANEL, step, 0)


def kernel(
    cls_ref, wave_ref, raw_hbm, data_hbm, rows_hbm, vals_hbm,
    raw, data, pk, kk, rr, qt, qin, mat, trow, dinv, cc, out, vt, vin, vals,
    load_sem, send_sem, recv_sem, store_sem,
):
    gx, gy = lax.axis_index("gx"), lax.axis_index("gy")
    size_x, size_y = lax.axis_size("gx"), lax.axis_size("gy")
    half_x, half_y = size_x // 2, size_y // 2
    col, row = gx // half_x, gy // half_y
    other_x, other_y = lax.rem(gx + half_x, size_x), lax.rem(gy + half_y, size_y)
    sib, diag, opp = (other_x, gy), (other_x, other_y), (gx, other_y)

    barrier = pltpu.get_barrier_semaphore()
    for peer in (sib, diag, opp):
        pl.semaphore_signal(barrier, inc=1, device_id=peer, device_id_type=MESH)

    low, high = pl.ds(0, 384), pl.ds(384, 384)
    loads = []
    for i, (r, c) in enumerate(((high, high), (high, low), (low, high), (low, low))):
        copy = pltpu.make_async_copy(raw_hbm.at[r, c], raw.at[r, c], load_sem.at[i])
        copy.start()
        loads.append(copy)
    data_copy = pltpu.make_async_copy(data_hbm, data, load_sem.at[4])
    data_copy.start()

    OWN, SIB, DIA, OPP = 0, 1, 2, 3
    place = {
        OWN: 2 * row + col,
        SIB: 2 * row + 1 - col,
        DIA: 2 * (1 - row) + 1 - col,
        OPP: 2 * (1 - row) + col,
    }
    flow = [0]
    sent = []

    def send(src, dst, peer):
        i = flow[0]
        flow[0] += 1
        copy = pltpu.make_async_remote_copy(
            src_ref=src, dst_ref=dst, send_sem=send_sem.at[i], recv_sem=recv_sem.at[i],
            device_id=peer, device_id_type=MESH,
        )
        copy.start()
        sent.append(copy)
        return copy

    def share(tile):
        return pl.ds(pl.multiple_of(place[tile] * SHARE, SHARE), SHARE)

    def khalf(tile, i):
        return pk.at[tile, pl.ds(0, 104) if i == 0 else pl.ds(104, 96), :]

    def rchunk(tile, start, size):
        return rr.at[tile, pl.ds(start, size), :]

    iota_r = lax.broadcasted_iota(jnp.int32, (T, T), 0)
    iota_c = lax.broadcasted_iota(jnp.int32, (T, T), 1)
    long_r = lax.broadcasted_iota(jnp.int32, (192, 384), 0)
    long_c = lax.broadcasted_iota(jnp.int32, (192, 384), 1)

    def diagonal(block):
        first = 4.0 + wave_ref[cls_ref[2 * block]]
        second = 4.0 + wave_ref[cls_ref[2 * block + 1]]
        return jnp.where(iota_r == iota_c, jnp.where(iota_r < 64, first, second), 0.0)

    loads[0].wait()
    for i in range(3):
        for j in range(3):
            block = raw[pl.ds(384 + T * i, T), pl.ds(384 + T * j, T)]
            mirror = raw[pl.ds(384 + T * j, T), pl.ds(384 + T * i, T)]
            summed = 0.5 * (block + mirror.T)
            if i == j:
                summed = summed + diagonal(3 + i)
            kk[OWN, pl.ds(T * i, T), pl.ds(T * j, T)] = summed

    shifted = pltpu.roll(kk[OWN, pl.ds(192, 192), :], 192, 1)
    in_y = long_c < 192
    pk[OWN, pl.ds(0, 192), :] = jnp.where(
        jnp.logical_and(in_y, long_c > long_r), shifted, kk[OWN, pl.ds(0, 192), :]
    )
    main = jnp.sum(jnp.where(long_c == long_r, shifted, 0.0), axis=0, keepdims=True)
    pk[OWN, pl.ds(192, 8), :] = jnp.broadcast_to(main, (8, 384))
    pl.semaphore_wait(barrier, 3)

    k_sib, k_dia = {}, {}
    for i in (0, 1):
        k_sib[i] = send(khalf(OWN, i), khalf(SIB, i), sib)
        k_dia[1 - i] = send(khalf(OWN, 1 - i), khalf(DIA, 1 - i), diag)

    loads[1].wait()
    loads[2].wait()
    for i in range(3):
        for j in range(3):
            block = raw[pl.ds(384 + T * i, T), pl.ds(T * j, T)]
            mirror = raw[pl.ds(T * j, T), pl.ds(384 + T * i, T)]
            rr[OWN, pl.ds(T * i, T), pl.ds(T * j, T)] = 0.5 * (block + mirror.T)
    data_copy.wait()
    qt[...] = lax.dot_general(
        data[...].T, rr[OWN], (((1,), (1,)), ((), ())),
        precision=highest, preferred_element_type=f32,
    )

    k_sib[0].wait_recv()
    k_opp = {0: send(khalf(SIB, 0), khalf(OPP, 0), diag)}
    k_dia[1].wait_recv()
    k_opp[1] = send(khalf(DIA, 1), khalf(OPP, 1), sib)

    q_in = [
        send(qt.at[share(OPP), :], qin.at[OPP], opp),
        send(qt.at[share(SIB), :], qin.at[SIB], sib),
        send(qt.at[share(DIA), :], qin.at[DIA], diag),
    ]

    def send_rows(start, size, peer, tile):
        return send(rchunk(OWN, start, size), rchunk(tile, start, size), peer)

    r_sib = [send_rows(0, T, sib, SIB)]
    r_dia = [send_rows(256, T, diag, DIA)]
    r_sib += [send_rows(T, 64, sib, SIB), send_rows(192, 192, sib, SIB)]
    r_dia += [send_rows(192, 64, diag, DIA), send_rows(0, 192, diag, DIA)]

    def unpack(tile):
        packed = pk[tile, pl.ds(0, 192), :]
        padded = jnp.concatenate([packed[T:, :], jnp.zeros((64, 384), f32)], axis=0)
        turned = []
        for i in range(3):
            lanes = slice(T * i, T * (i + 1))
            turned.append(
                jnp.concatenate(
                    [packed[:T, lanes].T, padded[:, lanes].T, jnp.zeros((T, T), f32)], axis=1
                )
            )
        turned = jnp.concatenate(turned, axis=0)
        top, bottom = turned[:192, :], turned[192:, :]
        kk[tile, pl.ds(0, 192), :] = jnp.where(
            jnp.logical_or(long_c >= 192, long_r >= long_c), packed, top
        )
        xx = jnp.where(
            long_r == long_c,
            jnp.broadcast_to(pk[tile, pl.ds(192, 1), :], (192, 384)),
            jnp.where(long_c > long_r, packed, top),
        )
        kk[tile, pl.ds(192, 192), :] = jnp.where(in_y, bottom, pltpu.roll(xx, 192, 1))

    def kblock(tile, i, j):
        return kk[tile, pl.ds(T * i, T), pl.ds(T * j, T)]

    k_sib[1].wait_recv()
    unpack(SIB)
    k_dia[0].wait_recv()
    unpack(DIA)
    for i in range(3):
        for j in range(3):
            row_y = iota_r + T * i < 192
            col_y = iota_c + T * j < 192
            own_block = kblock(OWN, i, j)
            dia_block = kblock(DIA, i, j)
            same = row_y == col_y
            yy = jnp.logical_and(row_y, col_y)
            yx = jnp.logical_and(row_y, jnp.logical_not(col_y))
            mat[j, pl.ds(T * i, T), :] = kblock(SIB, i, j) + jnp.where(
                same, jnp.where(yy, dia_block, own_block), 0.0
            )
            mat[3 + j, pl.ds(384 + T * i, T), :] = jnp.where(
                same, jnp.where(yy, own_block, dia_block), 0.0
            )
            mat[3 + j, pl.ds(T * i, T), :] = jnp.where(
                same, 0.0, jnp.where(yx, dia_block, own_block)
            )
            mat[j, pl.ds(384 + T * i, T), :] = jnp.where(
                same, 0.0, jnp.where(yx, own_block, dia_block)
            )

    def sweep(b, carry):
        start = pl.multiple_of(b * T, T)
        dinv[...] = mat[b, pl.ds(start, T), :]
        invert_tile(dinv)
        inverse = dinv[...]
        for j in range(6):
            trow[j] = product(inverse, mat[j, pl.ds(start, T), :])
        trow[b] = inverse
        column = mat[b]
        mat[b] = jnp.zeros((768, T), f32)
        for j in range(6):
            mat[j] = mat[j] - product(column, trow[j])
            mat[j, pl.ds(start, T), :] = trow[j]
        return carry

    lax.fori_loop(0, 3, sweep, 0)
    for i in range(2):
        k_opp[i].wait_recv()
    unpack(OPP)
    for i in range(3):
        for j in range(3):
            mat[3 + j, pl.ds(384 + T * i, T), :] += kblock(OPP, i, j)
    lax.fori_loop(3, 6, sweep, 0)


    for copy in q_in:
        copy.wait_recv()
    wide = lax.broadcasted_iota(jnp.int32, (SHARE, 384), 1) < 192
    own_q = qt[share(OWN), :]
    first = qin[SIB] + jnp.where(wide, qin[DIA], own_q)
    second = qin[OPP] + jnp.where(wide, own_q, qin[DIA])
    sides = jnp.concatenate([first, second], axis=1)
    solved = [-product(sides, mat[j]) for j in range(6)]
    near = jnp.concatenate(solved[:3], axis=1)
    far = jnp.concatenate(solved[3:], axis=1)
    vt[SIB] = near
    vt[OPP] = far
    vt[DIA] = jnp.where(wide, near, far)
    vin[share(OWN), :] = jnp.where(wide, far, near)

    v_in = [
        send(vt.at[OPP], vin.at[share(OWN), :], opp),
        send(vt.at[SIB], vin.at[share(OWN), :], sib),
        send(vt.at[DIA], vin.at[share(OWN), :], diag),
    ]
    r_opp = []
    r_sib[0].wait_recv()
    r_opp.append(send(rchunk(SIB, 0, T), rchunk(OPP, 0, T), diag))
    r_dia[0].wait_recv()
    r_opp.append(send(rchunk(DIA, 256, T), rchunk(OPP, 256, T), sib))
    r_sib[1].wait_recv()
    r_opp.append(send(rchunk(SIB, T, 64), rchunk(OPP, T, 64), diag))
    r_dia[1].wait_recv()
    r_opp.append(send(rchunk(DIA, 192, 64), rchunk(OPP, 192, 64), sib))

    own_rows = jnp.concatenate([rr[OWN, pl.ds(192, 192), :], rr[OWN, pl.ds(0, 192), :]], axis=0)
    for j in range(6):
        cc[j] = inner(own_rows, mat[j, pl.ds(192, 384), :])
    left = lax.broadcasted_iota(jnp.int32, (384, T), 1) < 64

    def parts(tile):
        if tile == SIB:
            return cc[0], cc[1], cc[2]
        if tile == OPP:
            return cc[3], cc[4], cc[5]
        if tile == DIA:
            return cc[0], jnp.where(left, cc[1], cc[4]), cc[5]
        return cc[3], jnp.where(left, cc[4], cc[1]), cc[2]

    loads[3].wait()
    for i in range(3):
        for j in range(3):
            block = raw[pl.ds(T * i, T), pl.ds(T * j, T)]
            mirror = raw[pl.ds(T * j, T), pl.ds(T * i, T)]
            summed = 0.5 * (block + mirror.T)
            if i == j:
                summed = summed + diagonal(i)
            out[OWN, pl.ds(T * i, T), pl.ds(T * j, T)] = summed

    stores = []

    def term(tile, j):
        return product(parts(tile)[j], rr[tile, pl.ds(T * j, T), :])

    def store(tile):
        copy = pltpu.make_async_copy(
            out.at[tile],
            rows_hbm.at[:, pl.ds(pl.multiple_of(place[tile] * 384, T), 384)],
            store_sem.at[tile],
        )
        copy.start()
        stores.append(copy)

    out[OWN] = out[OWN] - (term(OWN, 0) + term(OWN, 1) + term(OWN, 2))
    store(OWN)
    r_sib[2].wait_recv()
    out[SIB] = -(term(SIB, 0) + term(SIB, 1) + term(SIB, 2))
    store(SIB)
    r_dia[2].wait_recv()
    out[DIA] = -(term(DIA, 0) + term(DIA, 1) + term(DIA, 2))
    store(DIA)
    r_opp[0].wait_recv()
    r_opp[1].wait_recv()
    out[OPP] = -(term(OPP, 0) + term(OPP, 2))
    for copy in v_in:
        copy.wait_recv()
    vals[...] = vin[...].T
    copy = pltpu.make_async_copy(vals, vals_hbm, store_sem.at[4])
    copy.start()
    stores.append(copy)

    r_opp[2].wait_recv()
    r_opp[3].wait_recv()
    out[OPP] = out[OPP] - term(OPP, 1)
    store(OPP)

    for copy in sent:
        copy.wait_send()
    for copy in stores:
        copy.wait()


def body(leaf_raw, medium_class, wave_table, boundary_data):
    raw = pltpu.with_memory_space_constraint(leaf_raw[0, 0], pltpu.HBM)
    data = pltpu.with_memory_space_constraint(boundary_data[0, 0], pltpu.HBM)
    flows = 22
    rows, vals = pl.pallas_call(
        kernel,
        out_shape=(
            jax.ShapeDtypeStruct((384, 1536), f32),
            jax.ShapeDtypeStruct((384, T), f32),
        ),
        in_specs=[
            pl.BlockSpec(memory_space=pltpu.SMEM),
            pl.BlockSpec(memory_space=pltpu.SMEM),
            pl.BlockSpec(memory_space=pltpu.HBM),
            pl.BlockSpec(memory_space=pltpu.HBM),
        ],
        out_specs=(
            pl.BlockSpec(memory_space=pl.ANY),
            pl.BlockSpec(memory_space=pl.ANY),
        ),
        scratch_shapes=[
            pltpu.VMEM((768, 768), f32),
            pltpu.VMEM((384, T), f32),
            pltpu.VMEM((4, 200, 384), f32),
            pltpu.VMEM((4, 384, 384), f32),
            pltpu.VMEM((4, 384, 384), f32),
            pltpu.VMEM((T, 384), f32),
            pltpu.VMEM((4, SHARE, 384), f32),
            pltpu.VMEM((6, 768, T), f32),
            pltpu.VMEM((6, T, T), f32),
            pltpu.VMEM((T, T), f32),
            pltpu.VMEM((6, 384, T), f32),
            pltpu.VMEM((4, 384, 384), f32),
            pltpu.VMEM((4, SHARE, 384), f32),
            pltpu.VMEM((T, 384), f32),
            pltpu.VMEM((384, T), f32),
            pltpu.SemaphoreType.DMA((5,)),
            pltpu.SemaphoreType.DMA((flows,)),
            pltpu.SemaphoreType.DMA((flows,)),
            pltpu.SemaphoreType.DMA((5,)),
        ],
        compiler_params=pltpu.CompilerParams(
            collective_id=0, has_side_effects=True, vmem_limit_bytes=48 << 20
        ),
    )(
        pltpu.with_memory_space_constraint(medium_class[0, 0], pltpu.HBM),
        pltpu.with_memory_space_constraint(wave_table, pltpu.HBM),
        raw, data,
    )
    return rows[None, None], vals[None, None]


def solution(mesh):
    return jax.shard_map(
        body,
        mesh=mesh,
        in_specs=(P("gx", "gy", None, None), P("gx", "gy", None), P(), P("gx", "gy", None, None)),
        out_specs=(P("gx", "gy", None, None), P("gx", "gy", None, None)),
        check_vma=False,
    )
```
